128 devices in a mesh: aux: 4 (over x), pair: 32 (over z, y, core).
Axes of the slice: x: 4, y: 4, z: 4, core: 2. Of those that a mesh axis runs over, the one named last changes fastest.
Arguments:
- orbital_slabs: bfloat16 [128, 1024, 768], P('pair', 'aux'), may hold values from -2.5 to 2.5
- pno_maps: bfloat16 [512, 768, 256], P('pair'), may hold values from -0.21875 to 0.21875
- intersections: bfloat16 [512, 8, 256, 256], P('pair', 'aux'), may hold values from -0.375 to 0.375
- pno_energy: float32 [512, 256], P('pair'), may hold values from 0.25 to 2
- occ_energy: float32 [128], replicated, may hold values from -1 to -0.25
- pair_orbitals: int32 [512, 2], replicated, may hold values from 0 to 127, as said below
- partners: int32 [512, 8], replicated, may hold values from 0 to 511, as said below
- live: int32 [512], P('pair'), may hold values from 0 to 1, as said below
Outputs:
- amplitudes: bfloat16 [512, 256, 256], P('pair')
- pair_energy: float32 [512], P('pair')
The draws below stay inside these ranges and needn't reach their ends.
Inputs may be any that keep to these rules, and one draw needn't show every extreme that they name: `pair_orbitals`: each pair names two different orbitals. The pairs of one cluster of 16 slots (padding slots too) name at most one orbital of each block of 4 consecutive orbitals. `partners`: every partner is a live pair. All 128 partner entries of one cluster of 16 slots together name at most one pair of each cluster. In each cluster of 16 slots the live pairs come first and there is at least one; some cluster is full.
All inputs are finite; a program needn't handle non-finite values.
Results may differ from the reference program's by a relative error of at most 0.0066.
Values may be sent and summed in bfloat16 or wider, within the bound.
No kernel may reach another device: no remote copies, remote signals or barrier semaphores. Data moves between devices by JAX's collectives and lax.ppermute only.
A program may use at most 128 MiB of HBM per device.

```python
import math
import jax
import jax.numpy as jnp
from jax import lax

VIRT = 768
AUX = 1024
PNO = 256
PARTNERS = 8
ITERS = 2
ORB_DEV = 4
PAIR_DEV = 16
ORBITALS = 128
PAIRS = 512


def draw_tables(key):
    clusters = PAIRS // PAIR_DEV
    owners = ORBITALS // ORB_DEV
    keys = jax.random.split(jax.random.fold_in(key, 4242), 7)
    lowest = max(1, PAIR_DEV // 4)
    counts = jax.random.randint(keys[0], (clusters,), lowest, PAIR_DEV + 1)
    fullest = jax.random.randint(keys[1], (), 0, clusters)
    counts = jnp.where(jnp.arange(clusters) == fullest, PAIR_DEV, counts).astype(jnp.int32)
    slot_index = jnp.arange(PAIRS) % PAIR_DEV
    cluster_of = jnp.arange(PAIRS) // PAIR_DEV
    live_slots = (slot_index < counts[cluster_of]).astype(jnp.int32)
    orbital_pool = jnp.arange(owners)[None, :] * ORB_DEV + jax.random.randint(keys[2], (clusters, owners), 0, ORB_DEV)
    first_owner = jax.random.randint(keys[3], (PAIRS,), 0, owners)
    second_owner = (first_owner + 1 + jax.random.randint(keys[4], (PAIRS,), 0, owners - 1)) % owners
    orbitals = jnp.stack([orbital_pool[cluster_of, first_owner], orbital_pool[cluster_of, second_owner]], axis=1).astype(jnp.int32)
    chosen_slot = jax.random.randint(keys[5], (clusters, clusters), 0, counts[None, :])
    partner_source = jax.random.randint(keys[6], (PAIRS, PARTNERS), 0, clusters)
    partner_ids = partner_source * PAIR_DEV + chosen_slot[cluster_of[:, None], partner_source]
    return (orbitals, partner_ids.astype(jnp.int32), live_slots)


def draw_pair_orbitals(key, part):
    return draw_tables(key)[0]


def draw_partners(key, part):
    return draw_tables(key)[1]


def draw_live(key, part):
    return draw_tables(key)[2]


def block_scale(stream_key, dims, pieces, low, top_value):
    gain = 1.0
    for axis_at, blocks in pieces:
        heights = jax.random.uniform(jax.random.fold_in(jax.random.fold_in(stream_key, 6), axis_at), (blocks,), jnp.float32, low / len(pieces), top_value / len(pieces))
        gain = gain * jnp.repeat(jnp.exp(heights), dims[axis_at] // blocks).reshape((-1,) + (1,) * (len(dims) - 1 - axis_at))
    return gain


def scatter_about(rng, extent, width, bound, cuts=(), kind=jnp.bfloat16):
    entries = width * jax.random.normal(rng, extent, jnp.float32)
    if cuts:
        entries = entries * block_scale(rng, extent, cuts, -0.22, 0.18)
    return jnp.clip(entries, -bound, bound).astype(kind)


def setup_inputs(seed: int = 0) -> dict:
    key_of = jax.random.split(jax.random.key(seed), 9)
    orbital_slabs = scatter_about(key_of[0], (ORBITALS, AUX, VIRT), 0.18, 2.5, ((0, 32), (1, 4)))
    pno_maps = scatter_about(key_of[1], (PAIRS, VIRT, PNO), VIRT ** -0.5, 0.21875, ((0, 32),))
    intersections = scatter_about(key_of[2], (PAIRS, PARTNERS, PNO, PNO), PNO ** -0.5, 0.375, ((0, 32), (1, 4)))
    pno_energy = jnp.clip(jnp.exp(math.log(2.0) - 2.0794415 * jax.random.uniform(key_of[3], (PAIRS, PNO), jnp.float32) ** block_scale(key_of[3], (PAIRS, PNO), ((0, 32),), -0.2, 0.2)), 0.25, 2.0)
    occ_energy = jnp.clip(jax.random.uniform(key_of[4], (ORBITALS,), jnp.float32, -1.0, -0.25), -1.0, -0.25)
    pair_orbitals = draw_pair_orbitals(jax.random.fold_in(key_of[8], 71), 0)
    partners = draw_partners(jax.random.fold_in(key_of[8], 71), 0)
    live = draw_live(jax.random.fold_in(key_of[8], 71), 0)
    return dict(orbital_slabs=orbital_slabs, pno_maps=pno_maps, intersections=intersections, pno_energy=pno_energy, occ_energy=occ_energy, pair_orbitals=pair_orbitals, partners=partners, live=live)


damping = 0.7


def reference(orbital_slabs, pno_maps, intersections, pno_energy, occ_energy, pair_orbitals, partners, live):
    weights = live.astype(jnp.float32)[:, None, None]
    indices = jnp.arange(PAIRS, dtype=jnp.int32)

    def integrals(index):
        first = pair_orbitals[index, 0]
        second = pair_orbitals[index, 1]
        mapping = pno_maps[index]
        left = jnp.dot(orbital_slabs[first], mapping, preferred_element_type=jnp.float32).astype(jnp.bfloat16)
        right = jnp.dot(orbital_slabs[second], mapping, preferred_element_type=jnp.float32).astype(jnp.bfloat16)
        return jnp.dot(left.T, right, preferred_element_type=jnp.float32)

    coulomb = lax.map(integrals, indices)
    coulomb_half = coulomb.astype(jnp.bfloat16)
    occupied = occ_energy[pair_orbitals[:, 0]] + occ_energy[pair_orbitals[:, 1]]
    denominator = pno_energy[:, :, None] + pno_energy[:, None, :] - occupied[:, None, None]
    amplitude = -weights * coulomb / denominator
    for sweep in range(ITERS):
        amp_half = amplitude.astype(jnp.bfloat16)

        def coupling(index):
            fetched = amp_half[partners[index]].astype(jnp.float32)
            intersection = intersections[index].astype(jnp.float32)
            rotated = jnp.einsum("rab,rbc->rac", intersection, fetched)
            rotated = lax.optimization_barrier(rotated.astype(jnp.bfloat16)).astype(jnp.float32)
            return jnp.einsum("rac,rdc->ad", rotated, intersection)

        coupled = lax.map(coupling, indices)
        amp_wide = amp_half.astype(jnp.float32)
        product = jnp.einsum("pab,pcb->pac", amp_wide, coulomb_half.astype(jnp.float32))
        product = lax.optimization_barrier(product.astype(jnp.bfloat16)).astype(jnp.float32)
        quadratic = jnp.einsum("pac,pcd->pad", product, amp_wide) / PNO
        residual = coulomb + denominator * amplitude - coupled + quadratic
        amplitude = weights * (amplitude - damping * residual / denominator)
    energy = weights[:, 0, 0] * jnp.sum(coulomb * amplitude, axis=(1, 2))
    return amplitude.astype(jnp.bfloat16), energy
```

```python
import functools

import jax
import jax.numpy as jnp
from jax import lax
from jax.experimental import pallas as pl
from jax.experimental.pallas import tpu as pltpu
from jax.sharding import PartitionSpec as P

ITERS = 2
damping = 0.7
NX, NY, NZ, NC = 4, 4, 4, 2
BF, F32 = jnp.bfloat16, jnp.float32

SMEM = functools.partial(pl.BlockSpec, memory_space=pltpu.SMEM)
HBM = functools.partial(pl.BlockSpec, memory_space=pltpu.HBM)
VMEM = functools.partial(pl.BlockSpec, memory_space=pltpu.VMEM)


def rem(a, n):
    return lax.rem(a, jnp.int32(n))


def coords(cluster):
    return cluster // 8, rem(cluster // 2, 4), rem(cluster, 2)


def y_perm(step, flip):
    return [
        (z * 8 + y * 2 + c, z * 8 + (y + step) % NY * 2 + (c + flip) % NC)
        for z in range(NZ)
        for y in range(NY)
        for c in range(NC)
    ]


def z_perm(step, flip):
    return [
        (z * 8 + y * 2 + c, (z + step) % NZ * 8 + y * 2 + (c + flip) % NC)
        for z in range(NZ)
        for y in range(NY)
        for c in range(NC)
    ]


def shift_aux(value, step):
    return lax.ppermute(value, "aux", [(i, (i + step) % NX) for i in range(NX)])


def select_kernel(along_y, half, ids, table, own, back, ahead, far_low, far_high, *rest):
    outs, sem = rest[:8], rest[8]
    z, y, c = coords(ids[0])
    rows = own.shape[1] // 2
    waits = []
    for j in range(8):
        step, flip = j // 2, j % 2
        core = rem(c + flip, 2)
        if along_y:
            target = z * 8 + rem(y + step, NY) * 2 + core
        else:
            target = rem(z + step, NZ) * 8 + y * 2 + core
        for off in range(4):
            if along_y:
                block = rem(z + off, NZ) * 8 + y * 2 + c
            else:
                block = z * 8 + rem(y + off, NY) * 2 + c
            which = table[target, block]
            dst, s = outs[j].at[off], sem.at[j, off]
            if off == 0:
                src = own.at[which, pl.ds(half * rows, rows)]
                pltpu.make_async_copy(src, dst, s).start()
            elif off == 1:
                pltpu.make_async_copy(ahead.at[which], dst, s).start()
            elif off == 3:
                pltpu.make_async_copy(back.at[which], dst, s).start()
            else:

                @pl.when(which < 2)
                def _():
                    pltpu.make_async_copy(far_low.at[which], dst, s).start()

                @pl.when(which >= 2)
                def _():
                    pltpu.make_async_copy(far_high.at[which - 2], dst, s).start()

            waits.append(pltpu.make_async_copy(back.at[0], dst, s))
    for w in waits:
        w.wait()


def gather_half(along_y, half, ids, table, slabs):
    perm, cross = (z_perm, y_perm) if along_y else (y_perm, z_perm)
    rows = slabs.shape[1] // 2
    mine = slabs[:, half * rows : (half + 1) * rows]
    back = lax.ppermute(mine, "pair", perm(1, 0))
    ahead = lax.ppermute(mine, "pair", perm(3, 0))
    far_low = lax.ppermute(back[:2], "pair", perm(1, 0))
    far_high = lax.ppermute(ahead[2:], "pair", perm(3, 0))
    shape = jax.ShapeDtypeStruct((4, rows, slabs.shape[2]), slabs.dtype)
    outs = pl.pallas_call(
        functools.partial(select_kernel, along_y, half),
        out_shape=[shape] * 8,
        in_specs=[SMEM(), SMEM()] + [HBM()] * 5,
        out_specs=[HBM()] * 8,
        scratch_shapes=[pltpu.SemaphoreType.DMA((8, 4))],
        name="select_y" if along_y else "select_z",
    )(ids, table, slabs, back, ahead, far_low, far_high)
    order = [j for j in (4, 5, 2, 6, 3, 7, 1)]
    got = {0: outs[0]}
    for j in order:
        got[j] = lax.ppermute(outs[j], "pair", cross(j // 2, j % 2))
    return [got[j] for j in range(8)]


def split_rows(aux, tile, outs, index):
    for s, out in enumerate(outs):
        start = pl.multiple_of(rem(aux + s, NX) * 64, 64)
        out[index] = tile[pl.ds(start, 64), :].astype(out.dtype)


def coulomb_kernel(ids, orbitals, *rest):
    along_y, along_z, maps = rest[:8], rest[8:16], rest[16]
    outs = rest[17:21]
    slabs, mapped, tile, sem, map_sem = rest[21:]
    z, y, c = coords(ids[0])
    aux = ids[1]
    rows = 128

    def issue(p, _):
        pltpu.make_async_copy(maps.at[p], mapped.at[p], map_sem.at[p]).start()
        for side in range(2):
            block = orbitals[p * 2 + side] // 4
            bz, by, bc = coords(block)
            flip = rem(c + bc, 2)
            from_y = rem(y - by + NY, NY) * 2 + flip
            slot_y = rem(bz - z + NZ, NZ)
            from_z = rem(z - bz + NZ, NZ) * 2 + flip
            slot_z = rem(by - y + NY, NY)
            for half, (source, which, slot) in enumerate(
                ((along_y, from_y, slot_y), (along_z, from_z, slot_z))
            ):
                n = side * 2 + half
                dst = slabs.at[p, pl.ds(n * rows, rows)]
                for j in range(8):

                    @pl.when(which == j)
                    def _():
                        pltpu.make_async_copy(source[j].at[slot], dst, sem.at[p, n]).start()

        return 0

    lax.fori_loop(0, maps.shape[0], issue, 0)

    def compute(p, _):
        pltpu.make_async_copy(maps.at[p], mapped.at[p], map_sem.at[p]).wait()
        for n in range(4):
            dst = slabs.at[p, pl.ds(n * rows, rows)]
            pltpu.make_async_copy(along_y[0].at[0], dst, sem.at[p, n]).wait()
        both = jnp.dot(slabs[p], mapped[p], preferred_element_type=F32).astype(BF)
        tile[...] = lax.dot_general(
            both[:256], both[256:], (((0,), (0,)), ((), ())), preferred_element_type=F32
        )
        split_rows(aux, tile, outs, p)
        return 0

    lax.fori_loop(0, maps.shape[0], compute, 0)


def quarter_outs(pairs):
    return [jax.ShapeDtypeStruct((pairs, 64, 256), F32)] + [
        jax.ShapeDtypeStruct((pairs, 64, 256), BF)
    ] * 3


def send_tables(aux, names, send, amps, extra, outgoing, parts):
    def put(d, _):
        outgoing[d] = amps[send[d]]
        return 0

    lax.fori_loop(0, outgoing.shape[0], put, 0)
    for s, part in enumerate(parts):
        first = rem(aux + s, NX) * 4
        for n, array in enumerate(extra):
            part[n] = array[pl.ds(first, 4)]


def first_kernel(ids, send, live, own, r1, r2, r3, denominator, coulomb, amplitude, outgoing, *rest):
    parts, amps, halves = rest[:4], rest[4], rest[5]

    def one(p, _):
        total = own[p] + r1[p].astype(F32) + r2[p].astype(F32) + r3[p].astype(F32)
        weight = live[p].astype(F32)
        amp = -weight * total / denominator[p]
        coulomb[p] = total
        amplitude[p] = amp
        amps[p] = amp.astype(BF)
        halves[p] = total.astype(BF)
        return 0

    lax.fori_loop(0, own.shape[0], one, 0)
    send_tables(ids[1], None, send, amps, (amps, halves), outgoing, parts)


def updated(p, live, own, r1, r2, r3, coulomb, amplitude, denominator):
    net = own[p] + r1[p].astype(F32) + r2[p].astype(F32) + r3[p].astype(F32)
    weight = live[p].astype(F32)
    den, amp = denominator[p], amplitude[p]
    residual = coulomb[p] + den * amp - net
    return weight * (amp - damping * residual / den), weight


def sweep_kernel(ids, send, live, own, r1, r2, r3, denominator, coulomb, old, amplitude, outgoing, *rest):
    parts, amps = rest[:4], rest[4]

    def one(p, _):
        amp, _ = updated(p, live, own, r1, r2, r3, coulomb, old, denominator)
        amplitude[p] = amp
        amps[p] = amp.astype(BF)
        return 0

    lax.fori_loop(0, own.shape[0], one, 0)
    send_tables(ids[1], None, send, amps, (amps,), outgoing, parts)


def last_kernel(live, own, r1, r2, r3, denominator, coulomb, old, amps, energy):
    def one(p, _):
        amp, weight = updated(p, live, own, r1, r2, r3, coulomb, old, denominator)
        amps[p] = amp.astype(BF)
        part = jnp.sum(coulomb[p] * amp, axis=0, keepdims=True)
        total = jnp.sum(part, axis=1, keepdims=True) * weight
        energy[pl.ds(p, 1), :] = jnp.broadcast_to(total, (1, 128))
        return 0

    lax.fori_loop(0, own.shape[0], one, 0)


def couple_kernel(ids, slots, turned, rows_in, *rest):
    amp_parts, half_parts = rest[:4], rest[4:8]
    outs = rest[8:12]
    tile, amp_full, half_full = rest[12:]
    p = pl.program_id(0)
    aux = ids[1]
    start = pl.multiple_of(aux * 64, 64)
    first, second = [], []
    for k in range(8):
        holder, column = k // 2, k % 2
        piece = rows_in[slots[p * 8 + k]]
        square = turned[holder, 0, column]
        first.append(jnp.dot(piece, square, preferred_element_type=F32).astype(BF))
        second.append(turned[holder, 0, column, pl.ds(start, 64), :])
    tile[...] = lax.dot_general(
        jnp.concatenate(second, axis=0),
        jnp.concatenate(first, axis=0),
        (((0,), (0,)), ((), ())),
        preferred_element_type=F32,
    )

    @pl.when(p // 4 == aux)
    def _():
        n = rem(p, 4)
        for s in range(NX):
            at = pl.multiple_of(rem(aux - s + NX, NX) * 64, 64)
            amp_full[pl.ds(at, 64), :] = amp_parts[s][0, n]
            half_full[pl.ds(at, 64), :] = half_parts[s][half_parts[s].shape[0] - 1, n]
        amp = amp_full[...]
        product = lax.dot_general(
            amp, half_full[...], (((1,), (1,)), ((), ())), preferred_element_type=F32
        ).astype(BF)
        tile[...] -= jnp.dot(product, amp, preferred_element_type=F32) * (1.0 / 256.0)

    split_rows(aux, tile, outs, 0)


def join_kernel(ids, own, r1, r2, r3, out, sem):
    aux = ids[1]
    copies = []
    for s, part in enumerate((own, r1, r2, r3)):
        at = pl.multiple_of(rem(aux - s + NX, NX) * 64, 64)
        copies.append(pltpu.make_async_copy(part, out.at[:, pl.ds(at, 64), :], sem.at[s]))
    for copy in copies:
        copy.start()
    for copy in copies:
        copy.wait()


def on_device(
    orbital_slabs, pno_maps, intersections, pno_energy, occ_energy, pair_orbitals, partners, live
):
    clusters = lax.axis_size("pair")
    cluster = lax.axis_index("pair").astype(jnp.int32)
    aux = lax.axis_index("aux").astype(jnp.int32)
    pairs = pno_maps.shape[0]
    ids = jnp.stack([cluster, aux])

    turned = lax.all_gather(jnp.swapaxes(intersections, 2, 3), "aux", axis=0, tiled=False)

    wanted = pair_orbitals.reshape(clusters, 2 * pairs)
    blocks = jnp.arange(clusters, dtype=jnp.int32)
    table = jnp.max(
        jnp.where((wanted // 4)[:, :, None] == blocks[None, None, :], (wanted % 4)[:, :, None], 0),
        axis=1,
    )
    along_y = gather_half(True, 0, ids, table, orbital_slabs)
    along_z = gather_half(False, 1, ids, table, orbital_slabs)

    my_orbitals = lax.dynamic_slice_in_dim(pair_orbitals, cluster * pairs, pairs, 0)
    my_partners = lax.dynamic_slice_in_dim(partners, cluster * pairs, pairs, 0)
    slots = (my_partners // pairs).reshape(-1)
    refs = partners.reshape(clusters, -1)
    send = jnp.max(jnp.where(refs // pairs == cluster, refs % pairs, 0), axis=1)
    occupied = jnp.sum(jnp.take(occ_energy, my_orbitals), axis=1)
    my_rows = lax.dynamic_slice_in_dim(pno_energy, aux * 64, 64, 1)
    denominator = my_rows[:, :, None] + pno_energy[:, None, :] - occupied[:, None, None]

    quarters = quarter_outs(pairs)
    sums = pl.pallas_call(
        coulomb_kernel,
        out_shape=quarters,
        in_specs=[SMEM(), SMEM()] + [HBM()] * 17,
        out_specs=[VMEM()] * 4,
        scratch_shapes=[
            pltpu.VMEM((pairs, 512, 768), BF),
            pltpu.VMEM((pairs, 768, 256), BF),
            pltpu.VMEM((256, 256), F32),
            pltpu.SemaphoreType.DMA((pairs, 4)),
            pltpu.SemaphoreType.DMA((pairs,)),
        ],
        name="coulomb",
    )(ids, my_orbitals.reshape(-1), *along_y, *along_z, pno_maps)

    def exchanged(parts):
        return [parts[0]] + [shift_aux(parts[s], s) for s in (1, 2, 3)]

    wide = jax.ShapeDtypeStruct((pairs, 64, 256), F32)
    narrow = jax.ShapeDtypeStruct((pairs, 64, 256), BF)
    out_slots = jax.ShapeDtypeStruct((clusters, 64, 256), BF)

    def share(count):
        return [jax.ShapeDtypeStruct((count, 4, 64, 256), BF)] * 4

    got = exchanged(sums)
    coulomb, amplitude, outgoing, *parts = pl.pallas_call(
        first_kernel,
        out_shape=[wide, wide, out_slots] + share(2),
        in_specs=[SMEM()] * 3 + [VMEM()] * 5,
        out_specs=[VMEM()] * 7,
        scratch_shapes=[pltpu.VMEM((pairs, 64, 256), BF)] * 2,
        name="first",
    )(ids, send, live, *got, denominator)
    half_parts = None
    for sweep in range(ITERS):
        amp_parts = exchanged(parts)
        if sweep == 0:
            half_parts = amp_parts
        arrived = lax.all_to_all(outgoing, "pair", split_axis=0, concat_axis=0, tiled=True)
        amp_spec = pl.BlockSpec(amp_parts[0].shape, lambda p: (0, 0, 0, 0))
        half_spec = pl.BlockSpec(half_parts[0].shape, lambda p: (0, 0, 0, 0))
        sums = pl.pallas_call(
            couple_kernel,
            grid=(pairs,),
            out_shape=quarters,
            in_specs=[
                SMEM(),
                SMEM(),
                pl.BlockSpec((NX, 1, 2, 256, 256), lambda p: (0, p, 0, 0, 0)),
                pl.BlockSpec(arrived.shape, lambda p: (0, 0, 0)),
            ]
            + [amp_spec] * 4
            + [half_spec] * 4,
            out_specs=[pl.BlockSpec((1, 64, 256), lambda p: (p, 0, 0))] * 4,
            scratch_shapes=[
                pltpu.VMEM((256, 256), F32),
                pltpu.VMEM((256, 256), BF),
                pltpu.VMEM((256, 256), BF),
            ],
            name="couple",
        )(ids, slots, turned, arrived, *amp_parts, *half_parts)
        got = exchanged(sums)
        if sweep + 1 < ITERS:
            amplitude, outgoing, *parts = pl.pallas_call(
                sweep_kernel,
                out_shape=[wide, out_slots] + share(1),
                in_specs=[SMEM()] * 3 + [VMEM()] * 7,
                out_specs=[VMEM()] * 6,
                scratch_shapes=[pltpu.VMEM((pairs, 64, 256), BF)],
                name="sweep",
            )(ids, send, live, *got, denominator, coulomb, amplitude)
    final, energy = pl.pallas_call(
        last_kernel,
        out_shape=[narrow, jax.ShapeDtypeStruct((pairs, 128), F32)],
        in_specs=[SMEM()] + [VMEM()] * 7,
        out_specs=[VMEM()] * 2,
        name="last",
    )(live, *got, denominator, coulomb, amplitude)
    pieces = [final] + [shift_aux(final, s) for s in (1, 2, 3)]
    energy = lax.psum(energy[:, 0], "aux")
    result = pl.pallas_call(
        join_kernel,
        out_shape=jax.ShapeDtypeStruct((pairs, 256, 256), BF),
        in_specs=[SMEM()] + [HBM()] * 4,
        out_specs=HBM(),
        scratch_shapes=[pltpu.SemaphoreType.DMA((4,))],
        name="join",
    )(ids, *pieces)
    return (result, energy)


def solution(mesh):
    placed = (
        P("pair", "aux", None),
        P("pair", None, None),
        P("pair", "aux", None, None),
        P("pair", None),
        P(),
        P(),
        P(),
        P("pair"),
    )
    return jax.shard_map(
        on_device,
        mesh=mesh,
        in_specs=placed,
        out_specs=(P("pair", None, None), P("pair")),
        check_vma=False,
    )
```

```python
import functools

import jax
import jax.numpy as jnp
from jax import lax
from jax.experimental import pallas as pl
from jax.experimental.pallas import tpu as pltpu
from jax.sharding import PartitionSpec as P

ITERS = 2
damping = 0.7
NX, NY, NZ, NC = 4, 4, 4, 2
BF, F32 = jnp.bfloat16, jnp.float32

SMEM = functools.partial(pl.BlockSpec, memory_space=pltpu.SMEM)
HBM = functools.partial(pl.BlockSpec, memory_space=pltpu.HBM)
VMEM = functools.partial(pl.BlockSpec, memory_space=pltpu.VMEM)


def rem(a, n):
    return lax.rem(a, jnp.int32(n))


def coords(cluster):
    return cluster // 8, rem(cluster // 2, 4), rem(cluster, 2)


def y_perm(step, flip):
    return [
        (z * 8 + y * 2 + c, z * 8 + (y + step) % NY * 2 + (c + flip) % NC)
        for z in range(NZ)
        for y in range(NY)
        for c in range(NC)
    ]


def z_perm(step, flip):
    return [
        (z * 8 + y * 2 + c, (z + step) % NZ * 8 + y * 2 + (c + flip) % NC)
        for z in range(NZ)
        for y in range(NY)
        for c in range(NC)
    ]


def shift_aux(value, step):
    return lax.ppermute(value, "aux", [(i, (i + step) % NX) for i in range(NX)])


def select_kernel(along_y, ids, table, own, back, ahead, far_low, far_high, *rest):
    outs, sem = rest[:8], rest[8]
    z, y, c = coords(ids[0])
    waits = []
    for j in range(8):
        step, flip = j // 2, j % 2
        core = rem(c + flip, 2)
        if along_y:
            target = z * 8 + rem(y + step, NY) * 2 + core
        else:
            target = rem(z + step, NZ) * 8 + y * 2 + core
        for off in range(4):
            if along_y:
                block = rem(z + off, NZ) * 8 + y * 2 + c
            else:
                block = z * 8 + rem(y + off, NY) * 2 + c
            which = table[target, block]
            dst, s = outs[j].at[off], sem.at[j, off]
            if off == 0:
                pltpu.make_async_copy(own.at[which], dst, s).start()
            elif off == 1:
                pltpu.make_async_copy(ahead.at[which], dst, s).start()
            elif off == 3:
                pltpu.make_async_copy(back.at[which], dst, s).start()
            else:

                @pl.when(which < 2)
                def _():
                    pltpu.make_async_copy(far_low.at[which], dst, s).start()

                @pl.when(which >= 2)
                def _():
                    pltpu.make_async_copy(far_high.at[which - 2], dst, s).start()

            waits.append(pltpu.make_async_copy(back.at[0], dst, s))
    for w in waits:
        w.wait()


def gather_half(along_y, half, ids, table, slabs):
    perm, cross = (z_perm, y_perm) if along_y else (y_perm, z_perm)
    rows = slabs.shape[1] // 2
    mine = slabs[:, half * rows : (half + 1) * rows]
    back = lax.ppermute(mine, "pair", perm(1, 0))
    ahead = lax.ppermute(mine, "pair", perm(3, 0))
    far_low = lax.ppermute(back[:2], "pair", perm(1, 0))
    far_high = lax.ppermute(ahead[2:], "pair", perm(3, 0))
    shape = jax.ShapeDtypeStruct((4, rows, slabs.shape[2]), slabs.dtype)
    outs = pl.pallas_call(
        functools.partial(select_kernel, along_y),
        out_shape=[shape] * 8,
        in_specs=[SMEM(), SMEM()] + [VMEM()] * 5,
        out_specs=[HBM()] * 8,
        scratch_shapes=[pltpu.SemaphoreType.DMA((8, 4))],
        name="select_y" if along_y else "select_z",
    )(ids, table, mine, back, ahead, far_low, far_high)
    order = [j for j in (4, 5, 2, 6, 3, 7, 1)]
    got = {0: outs[0]}
    for j in order:
        got[j] = lax.ppermute(outs[j], "pair", cross(j // 2, j % 2))
    return [got[j] for j in range(8)]


def split_rows(aux, tile, outs, index):
    for s, out in enumerate(outs):
        start = pl.multiple_of(rem(aux + s, NX) * 64, 64)
        out[index] = tile[pl.ds(start, 64), :].astype(out.dtype)


def coulomb_kernel(ids, orbitals, *rest):
    along_y, along_z, maps = rest[:8], rest[8:16], rest[16]
    outs = rest[17:21]
    slabs, mapped, tile, sem, map_sem = rest[21:]
    z, y, c = coords(ids[0])
    aux = ids[1]
    rows = 128

    def issue(p, _):
        pltpu.make_async_copy(maps.at[p], mapped.at[p], map_sem.at[p]).start()
        for side in range(2):
            block = orbitals[p * 2 + side] // 4
            bz, by, bc = coords(block)
            flip = rem(c + bc, 2)
            from_y = rem(y - by + NY, NY) * 2 + flip
            slot_y = rem(bz - z + NZ, NZ)
            from_z = rem(z - bz + NZ, NZ) * 2 + flip
            slot_z = rem(by - y + NY, NY)
            for half, (source, which, slot) in enumerate(
                ((along_y, from_y, slot_y), (along_z, from_z, slot_z))
            ):
                n = side * 2 + half
                dst = slabs.at[p, pl.ds(n * rows, rows)]
                for j in range(8):

                    @pl.when(which == j)
                    def _():
                        pltpu.make_async_copy(source[j].at[slot], dst, sem.at[p, n]).start()

        return 0

    lax.fori_loop(0, maps.shape[0], issue, 0)

    def compute(p, _):
        pltpu.make_async_copy(maps.at[p], mapped.at[p], map_sem.at[p]).wait()
        for n in range(4):
            dst = slabs.at[p, pl.ds(n * rows, rows)]
            pltpu.make_async_copy(along_y[0].at[0], dst, sem.at[p, n]).wait()
        both = jnp.dot(slabs[p], mapped[p], preferred_element_type=F32).astype(BF)
        tile[...] = lax.dot_general(
            both[:256], both[256:], (((0,), (0,)), ((), ())), preferred_element_type=F32
        )
        split_rows(aux, tile, outs, p)
        return 0

    lax.fori_loop(0, maps.shape[0], compute, 0)


def quarter_outs(pairs):
    return [jax.ShapeDtypeStruct((pairs, 64, 256), F32)] + [
        jax.ShapeDtypeStruct((pairs, 64, 256), BF)
    ] * 3


def send_tables(aux, names, send, amps, extra, outgoing, parts):
    def put(d, _):
        outgoing[d] = amps[send[d]]
        return 0

    lax.fori_loop(0, outgoing.shape[0], put, 0)
    for s, part in enumerate(parts):
        first = rem(aux + s, NX) * 4
        for n, array in enumerate(extra):
            part[n] = array[pl.ds(first, 4)]


def first_kernel(ids, send, live, own, r1, r2, r3, denominator, coulomb, amplitude, outgoing, *rest):
    parts, amps, halves = rest[:4], rest[4], rest[5]

    def one(p, _):
        total = own[p] + r1[p].astype(F32) + r2[p].astype(F32) + r3[p].astype(F32)
        weight = live[p].astype(F32)
        amp = -weight * total / denominator[p]
        coulomb[p] = total
        amplitude[p] = amp
        amps[p] = amp.astype(BF)
        halves[p] = total.astype(BF)
        return 0

    lax.fori_loop(0, own.shape[0], one, 0)
    send_tables(ids[1], None, send, amps, (amps, halves), outgoing, parts)


def updated(p, live, own, r1, r2, r3, coulomb, amplitude, denominator):
    net = own[p] + r1[p].astype(F32) + r2[p].astype(F32) + r3[p].astype(F32)
    weight = live[p].astype(F32)
    den, amp = denominator[p], amplitude[p]
    residual = coulomb[p] + den * amp - net
    return weight * (amp - damping * residual / den), weight


def sweep_kernel(ids, send, live, own, r1, r2, r3, denominator, coulomb, old, amplitude, outgoing, *rest):
    parts, amps = rest[:4], rest[4]

    def one(p, _):
        amp, _ = updated(p, live, own, r1, r2, r3, coulomb, old, denominator)
        amplitude[p] = amp
        amps[p] = amp.astype(BF)
        return 0

    lax.fori_loop(0, own.shape[0], one, 0)
    send_tables(ids[1], None, send, amps, (amps,), outgoing, parts)


def last_kernel(live, own, r1, r2, r3, denominator, coulomb, old, amps, energy):
    def one(p, _):
        amp, weight = updated(p, live, own, r1, r2, r3, coulomb, old, denominator)
        amps[p] = amp.astype(BF)
        part = jnp.sum(coulomb[p] * amp, axis=0, keepdims=True)
        total = jnp.sum(part, axis=1, keepdims=True) * weight
        energy[pl.ds(p, 1), :] = jnp.broadcast_to(total, (1, 128))
        return 0

    lax.fori_loop(0, own.shape[0], one, 0)


def couple_kernel(ids, slots, turned, rows_in, *rest):
    amp_parts, half_parts = rest[:4], rest[4:8]
    outs = rest[8:12]
    tile, amp_full, half_full = rest[12:]
    p = pl.program_id(0)
    aux = ids[1]
    start = pl.multiple_of(aux * 64, 64)
    first, second = [], []
    for k in range(8):
        holder, column = k // 2, k % 2
        piece = rows_in[slots[p * 8 + k]]
        square = turned[holder, 0, column]
        first.append(jnp.dot(piece, square, preferred_element_type=F32).astype(BF))
        second.append(turned[holder, 0, column, pl.ds(start, 64), :])
    tile[...] = lax.dot_general(
        jnp.concatenate(second, axis=0),
        jnp.concatenate(first, axis=0),
        (((0,), (0,)), ((), ())),
        preferred_element_type=F32,
    )

    @pl.when(p // 4 == aux)
    def _():
        n = rem(p, 4)
        for s in range(NX):
            at = pl.multiple_of(rem(aux - s + NX, NX) * 64, 64)
            amp_full[pl.ds(at, 64), :] = amp_parts[s][0, n]
            half_full[pl.ds(at, 64), :] = half_parts[s][half_parts[s].shape[0] - 1, n]
        amp = amp_full[...]
        product = lax.dot_general(
            amp, half_full[...], (((1,), (1,)), ((), ())), preferred_element_type=F32
        ).astype(BF)
        tile[...] -= jnp.dot(product, amp, preferred_element_type=F32) * (1.0 / 256.0)

    split_rows(aux, tile, outs, 0)


def join_kernel(ids, own, r1, r2, r3, out, sem):
    aux = ids[1]
    copies = []
    for s, part in enumerate((own, r1, r2, r3)):
        at = pl.multiple_of(rem(aux - s + NX, NX) * 64, 64)
        copies.append(pltpu.make_async_copy(part, out.at[:, pl.ds(at, 64), :], sem.at[s]))
    for copy in copies:
        copy.start()
    for copy in copies:
        copy.wait()


def on_device(
    orbital_slabs, pno_maps, intersections, pno_energy, occ_energy, pair_orbitals, partners, live
):
    clusters = lax.axis_size("pair")
    cluster = lax.axis_index("pair").astype(jnp.int32)
    aux = lax.axis_index("aux").astype(jnp.int32)
    pairs = pno_maps.shape[0]
    ids = jnp.stack([cluster, aux])

    turned = lax.all_gather(jnp.swapaxes(intersections, 2, 3), "aux", axis=0, tiled=False)

    wanted = pair_orbitals.reshape(clusters, 2 * pairs)
    blocks = jnp.arange(clusters, dtype=jnp.int32)
    table = jnp.max(
        jnp.where((wanted // 4)[:, :, None] == blocks[None, None, :], (wanted % 4)[:, :, None], 0),
        axis=1,
    )
    along_y = gather_half(True, 0, ids, table, orbital_slabs)
    along_z = gather_half(False, 1, ids, table, orbital_slabs)

    my_orbitals = lax.dynamic_slice_in_dim(pair_orbitals, cluster * pairs, pairs, 0)
    my_partners = lax.dynamic_slice_in_dim(partners, cluster * pairs, pairs, 0)
    slots = (my_partners // pairs).reshape(-1)
    refs = partners.reshape(clusters, -1)
    send = jnp.max(jnp.where(refs // pairs == cluster, refs % pairs, 0), axis=1)
    occupied = jnp.sum(jnp.take(occ_energy, my_orbitals), axis=1)
    my_rows = lax.dynamic_slice_in_dim(pno_energy, aux * 64, 64, 1)
    denominator = my_rows[:, :, None] + pno_energy[:, None, :] - occupied[:, None, None]

    quarters = quarter_outs(pairs)
    sums = pl.pallas_call(
        coulomb_kernel,
        out_shape=quarters,
        in_specs=[SMEM(), SMEM()] + [HBM()] * 17,
        out_specs=[VMEM()] * 4,
        scratch_shapes=[
            pltpu.VMEM((pairs, 512, 768), BF),
            pltpu.VMEM((pairs, 768, 256), BF),
            pltpu.VMEM((256, 256), F32),
            pltpu.SemaphoreType.DMA((pairs, 4)),
            pltpu.SemaphoreType.DMA((pairs,)),
        ],
        name="coulomb",
    )(ids, my_orbitals.reshape(-1), *along_y, *along_z, pno_maps)

    def exchanged(parts):
        return [parts[0]] + [shift_aux(parts[s], s) for s in (1, 2, 3)]

    wide = jax.ShapeDtypeStruct((pairs, 64, 256), F32)
    narrow = jax.ShapeDtypeStruct((pairs, 64, 256), BF)
    out_slots = jax.ShapeDtypeStruct((clusters, 64, 256), BF)

    def share(count):
        return [jax.ShapeDtypeStruct((count, 4, 64, 256), BF)] * 4

    got = exchanged(sums)
    coulomb, amplitude, outgoing, *parts = pl.pallas_call(
        first_kernel,
        out_shape=[wide, wide, out_slots] + share(2),
        in_specs=[SMEM()] * 3 + [VMEM()] * 5,
        out_specs=[VMEM()] * 7,
        scratch_shapes=[pltpu.VMEM((pairs, 64, 256), BF)] * 2,
        name="first",
    )(ids, send, live, *got, denominator)
    half_parts = None
    for sweep in range(ITERS):
        amp_parts = exchanged(parts)
        if sweep == 0:
            half_parts = amp_parts
        arrived = lax.all_to_all(outgoing, "pair", split_axis=0, concat_axis=0, tiled=True)
        amp_spec = pl.BlockSpec(amp_parts[0].shape, lambda p: (0, 0, 0, 0))
        half_spec = pl.BlockSpec(half_parts[0].shape, lambda p: (0, 0, 0, 0))
        sums = pl.pallas_call(
            couple_kernel,
            grid=(pairs,),
            out_shape=quarters,
            in_specs=[
                SMEM(),
                SMEM(),
                pl.BlockSpec((NX, 1, 2, 256, 256), lambda p: (0, p, 0, 0, 0)),
                pl.BlockSpec(arrived.shape, lambda p: (0, 0, 0)),
            ]
            + [amp_spec] * 4
            + [half_spec] * 4,
            out_specs=[pl.BlockSpec((1, 64, 256), lambda p: (p, 0, 0))] * 4,
            scratch_shapes=[
                pltpu.VMEM((256, 256), F32),
                pltpu.VMEM((256, 256), BF),
                pltpu.VMEM((256, 256), BF),
            ],
            name="couple",
        )(ids, slots, turned, arrived, *amp_parts, *half_parts)
        got = exchanged(sums)
        if sweep + 1 < ITERS:
            amplitude, outgoing, *parts = pl.pallas_call(
                sweep_kernel,
                out_shape=[wide, out_slots] + share(1),
                in_specs=[SMEM()] * 3 + [VMEM()] * 7,
                out_specs=[VMEM()] * 6,
                scratch_shapes=[pltpu.VMEM((pairs, 64, 256), BF)],
                name="sweep",
            )(ids, send, live, *got, denominator, coulomb, amplitude)
    final, energy = pl.pallas_call(
        last_kernel,
        out_shape=[narrow, jax.ShapeDtypeStruct((pairs, 128), F32)],
        in_specs=[SMEM()] + [VMEM()] * 7,
        out_specs=[VMEM()] * 2,
        name="last",
    )(live, *got, denominator, coulomb, amplitude)
    pieces = [final] + [shift_aux(final, s) for s in (1, 2, 3)]
    energy = lax.psum(energy[:, 0], "aux")
    result = pl.pallas_call(
        join_kernel,
        out_shape=jax.ShapeDtypeStruct((pairs, 256, 256), BF),
        in_specs=[SMEM()] + [VMEM()] * 4,
        out_specs=HBM(),
        scratch_shapes=[pltpu.SemaphoreType.DMA((4,))],
        name="join",
    )(ids, *pieces)
    return (result, energy)


def solution(mesh):
    placed = (
        P("pair", "aux", None),
        P("pair", None, None),
        P("pair", "aux", None, None),
        P("pair", None),
        P(),
        P(),
        P(),
        P("pair"),
    )
    return jax.shard_map(
        on_device,
        mesh=mesh,
        in_specs=placed,
        out_specs=(P("pair", None, None), P("pair")),
        check_vma=False,
    )
```
